32 devices in a mesh: param: 8 (over z, x), ex: 4 (over y, core).
Axes of the slice: x: 2, y: 2, z: 4, core: 2. Of those that a mesh axis runs over, the one named last changes fastest.
Arguments:
- gradients: float32 [256, 32768], P('ex', 'param')
- m_state: float32 [32768], P('param'), may hold values from -0.6 to 0.6
- v_state: float32 [32768], P('param'), may hold values from 0.001 to 0.1
- row_seeds: int32 [32768], P('param'), may hold values from 1 to 2999999
- col_seeds: int32 [8192], replicated, may hold values from 1 to 2999999
- group_of: int32 [256], replicated, may hold values from 0 to 56, as said below
Outputs:
- features: float32 [256, 8192], P('ex', 'param')
- scores: float32 [256, 57], P('ex')
The draws below stay inside these ranges and needn't reach their ends.
Inputs may be any that keep to these rules, and one draw needn't show every extreme that they name: `group_of`: every one of the 57 subtasks holds at least one example.
All inputs are finite; a program needn't handle non-finite values.
Results may differ from the reference program's by a relative error of at most 0.0029.
Values sent between devices are 32-bit elements; how exact they have to be, the bound alone decides.
No kernel may reach another device: no remote copies, remote signals or barrier semaphores. Data moves between devices by JAX's collectives and lax.ppermute only.
A program may use at most 64 MiB of HBM per device.

```python
import math
import jax
import jax.numpy as jnp
from jax import lax

K = 8192
GROUPS = 57
EXAMPLES = 256
PARAMS = 32768


def draw_gradients(key, part):
    scale_key = jax.random.fold_in(key, 11)
    noise_key = jax.random.fold_in(key, 12)
    scales = jnp.exp(jax.random.uniform(scale_key, (EXAMPLES, 1), jnp.float32, jnp.log(0.3), jnp.log(3.0)))
    noise = jax.random.normal(noise_key, (EXAMPLES, PARAMS), jnp.float32)
    return noise * scales


def draw_group_of(key, part):
    rest_key = jax.random.fold_in(key, 21)
    order_key = jax.random.fold_in(key, 22)
    rest = jax.random.randint(rest_key, (EXAMPLES - GROUPS,), 0, GROUPS, jnp.int32)
    labels = jnp.concatenate([jnp.arange(GROUPS, dtype=jnp.int32), rest])
    return jax.random.permutation(order_key, labels)


def plant(entries, stream_key, least, largest):
    longest = entries.shape.index(max(entries.shape))
    spots = []
    for shift in (0, 1):
        where = [jax.random.randint(jax.random.fold_in(stream_key, axis), (), 0, length) for axis, length in enumerate(entries.shape)]
        where[longest] = (where[longest] + shift) % entries.shape[longest]
        spots.append(tuple(where))
    return entries.at[spots[0]].set(least).at[spots[1]].set(largest)


def steps_of(stream_key, dims, shards, least, largest):
    gain = 1.0
    for axis_at, blocks in shards:
        draws = jax.random.uniform(jax.random.fold_in(jax.random.fold_in(stream_key, 6), axis_at), (blocks,), jnp.float32, least / len(shards), largest / len(shards))
        gain = gain * jnp.repeat(jnp.exp(draws), dims[axis_at] // blocks).reshape((-1,) + (1,) * (len(dims) - 1 - axis_at))
    return gain


def centred(key, shape, deviation, limit, shards=(), kind=jnp.bfloat16):
    drawn = deviation * jax.random.normal(key, shape, jnp.float32)
    if shards:
        drawn = drawn * steps_of(key, shape, shards, -0.22, 0.18)
    return jnp.clip(drawn, -limit, limit).astype(kind)


def setup_inputs(seed: int = 0) -> dict:
    keys = jax.random.split(jax.random.key(seed), 7)
    gradients = draw_gradients(jax.random.fold_in(keys[6], 71), 0)
    m_state = centred(keys[1], (PARAMS,), 0.1, 0.6, ((0, 8),), jnp.float32)
    v_state = jnp.clip(jnp.exp(math.log(0.1) - 4.6051702 * jax.random.uniform(keys[2], (PARAMS,), jnp.float32) ** steps_of(keys[2], (PARAMS,), ((0, 8),), -0.2, 0.2)), 0.001, 0.1)
    row_seeds = plant(jax.random.randint(keys[3], (PARAMS,), 1, 3000000), jax.random.fold_in(keys[3], 1), 1, 2999999).astype(jnp.int32)
    col_seeds = plant(jax.random.randint(keys[4], (K,), 1, 3000000), jax.random.fold_in(keys[4], 1), 1, 2999999).astype(jnp.int32)
    group_of = draw_group_of(jax.random.fold_in(keys[6], 71), 0)
    return dict(gradients=gradients, m_state=m_state, v_state=v_state, row_seeds=row_seeds, col_seeds=col_seeds, group_of=group_of)


def hashed_signs(row_part, col_part):
    hashed = row_part[:, None] * col_part[None, :]
    hashed = hashed ^ hashed >> 15
    hashed = hashed * jnp.int32(739982445)
    hashed = hashed ^ hashed >> 13
    return (1 - 2 * (hashed >> 11 & 1)).astype(jnp.bfloat16)

def reference(gradients, m_state, v_state, row_seeds, col_seeds, group_of):
    first_moment = 0.9 * m_state[None, :] + 0.1 * gradients
    second_moment = 0.999 * v_state[None, :] + 0.001 * gradients * gradients
    update = (first_moment / (jnp.sqrt(second_moment) + 1e-08)).astype(jnp.bfloat16)
    block_width = min(4096, PARAMS)
    blocks = PARAMS // block_width

    def accumulate(summed, block_index):
        begin_at = (block_index * block_width).astype(jnp.int32)
        seed_rows = lax.dynamic_slice_in_dim(row_seeds, begin_at, block_width)
        columns = lax.dynamic_slice_in_dim(update, begin_at, block_width, 1)
        return (summed + jnp.dot(columns, hashed_signs(seed_rows, col_seeds), preferred_element_type=jnp.float32), None)
    projected, unused = lax.scan(accumulate, jnp.zeros((EXAMPLES, K), jnp.float32), jnp.arange(blocks, dtype=jnp.int32))
    root_mean = jnp.sqrt(lax.optimization_barrier(jnp.mean(projected * projected, axis=1, keepdims=True)) + 1e-06)
    features = projected / root_mean
    products = jnp.dot(features, features.T, precision=lax.Precision.HIGHEST)
    onehot = (group_of[:, None] == jnp.arange(GROUPS, dtype=jnp.int32)[None, :]).astype(jnp.float32)
    counts = lax.optimization_barrier(jnp.sum(onehot, axis=0))
    scores = jnp.dot(products, onehot, precision=lax.Precision.HIGHEST) / (counts[None, :] * K)
    return (features, scores)
```

```python
import functools
import jax
import jax.numpy as jnp
from jax import lax
from jax.experimental import pallas as pl
from jax.experimental.pallas import tpu as pltpu
from jax.sharding import PartitionSpec as P

GROUPS = 57
LANES = 64
HIGHEST = lax.Precision.HIGHEST


def swap(value, axis, bits):
    return lax.ppermute(value, axis, [(i, i ^ bits) for i in range(lax.axis_size(axis))])


def wrapped(value):
    value &= 0xFFFFFFFF
    return jnp.int32(value - (1 << 32) if value >> 31 else value)


def hashed_signs(row_part, col_part):
    hashed = row_part * col_part
    hashed = hashed ^ hashed >> 15
    hashed = hashed * wrapped(739982445 << 7)
    hashed = hashed ^ hashed << 13
    return jnp.where(hashed < 0, jnp.bfloat16(-1), jnp.bfloat16(1))


def gather_kernel(own_ref, other_ref, both_ref):
    here = own_ref.shape[0]
    side = lax.axis_index("ex") % 2
    both_ref[pl.ds(pl.multiple_of(side * here, here), here), :] = own_ref[...].astype(jnp.bfloat16)
    both_ref[pl.ds(pl.multiple_of((1 - side) * here, here), here), :] = other_ref[...].astype(jnp.bfloat16)


def project_kernel(update_ref, rows_ref, cols_ref, out_ref, *, order, depth):
    own = lax.axis_index("param")
    side = lax.axis_index("ex") % 2
    width = out_ref.shape[2]
    strip = min(width, 256)
    steps = update_ref.shape[1] // depth
    for slot, relative in enumerate(order):
        at = (own ^ relative) * 2 + side

        def step(index, carry):
            begin = pl.multiple_of(index * depth, depth)
            update = update_ref[:, pl.ds(begin, depth)]
            seeds = rows_ref[pl.ds(begin, depth), :]
            seeds = jnp.tile(seeds, (1, strip // 128)) if strip > 128 else seeds[:, :strip]
            for left in range(0, width, strip):
                cols = cols_ref[pl.ds(at, 1), left : left + strip]
                part = jnp.dot(update, hashed_signs(seeds, cols), preferred_element_type=jnp.float32)
                view = out_ref.at[slot, :, left : left + strip]

                @pl.when(index == 0)
                def _():
                    view[...] = part

                @pl.when(index > 0)
                def _():
                    view[...] += part

            return carry

        lax.fori_loop(0, steps, step, 0)


def square_kernel(a_ref, b_ref, c_ref, d_ref, projected_ref, squares_ref):
    projected = a_ref[0] + b_ref[0] + c_ref[0] + d_ref[0]
    projected_ref[...] = projected
    ones = jnp.ones((8, projected.shape[1]), jnp.float32)
    squares_ref[...] = lax.dot_general(
        ones, projected * projected, (((1,), (1,)), ((), ())), precision=HIGHEST
    )


def score_kernel(squares_ref, groups_ref, own_ref, *refs, features_total):
    others, (feat_ref, feat_send_ref, score_ref, score_send_ref, roots) = refs[:-5], refs[-5:]
    rows = own_ref.shape[0]
    here = rows // 2
    pairs = 1 + len(others)
    me = lax.axis_index("ex")
    pair, side = me // 2, me % 2
    for y in range(pairs):
        total = jnp.zeros((8, rows), jnp.float32)
        for slot in range(squares_ref.shape[0]):
            if slot % (2 * pairs) // 2 == y:
                total = total + squares_ref[slot]
        roots[y * 8 : y * 8 + 8, :] = jnp.sqrt(total * (1.0 / features_total) + 1e-06)
    row = roots[pl.ds(pl.multiple_of(pair * 8, 8), 1), :]
    column = jnp.transpose(jnp.broadcast_to(row, (rows, rows)))[:, :1]
    own = own_ref[...]
    summed = jnp.zeros((rows, LANES), jnp.float32)
    counts = jnp.zeros((8, LANES), jnp.float32)
    for shift in range(pairs):
        there = (pair + shift) % pairs
        value = own if shift == 0 else others[shift - 1][...]
        products = lax.dot_general(own, value, (((1,), (1,)), ((), ())), precision=HIGHEST)
        products = products / roots[pl.ds(pl.multiple_of(there * 8, 8), 1), :]
        groups = groups_ref[pl.ds(there, 1), :]
        onehot = (lax.broadcasted_iota(jnp.int32, (LANES, rows), 0) == groups).astype(jnp.float32)
        summed = summed + lax.dot_general(products, onehot, (((1,), (1,)), ((), ())), precision=HIGHEST)
        counts = counts + lax.dot_general(
            jnp.ones((8, rows), jnp.float32), onehot, (((1,), (1,)), ((), ())), precision=HIGHEST
        )
    scale = jnp.maximum(counts[:1], 1.0) * features_total
    scores = summed / column / scale
    feats = own / column
    half = here // 2
    for target, target_score, wanted in ((feat_ref, score_ref, 0), (feat_send_ref, score_send_ref, 1)):
        first = side == wanted
        target[...] = jnp.where(first, feats[:here], feats[here:])
        chosen = jnp.where(first, scores[:here], scores[here:])
        target_score[...] = jnp.concatenate([chosen[:half], chosen[half:]], axis=1)


def finish_kernel(score_ref, out_ref):
    half = score_ref.shape[1]
    total = score_ref[0]
    for slot in range(1, score_ref.shape[0]):
        total = total + score_ref[slot]
    out_ref[:half, :] = total[:, :GROUPS]
    out_ref[half:, :] = total[:, LANES : LANES + GROUPS]


def shards(gradients, m_state, v_state, row_seeds, col_seeds, group_of):
    first_moment = 0.9 * m_state[None, :] + 0.1 * gradients
    second_moment = 0.999 * v_state[None, :] + 0.001 * gradients * gradients
    update = first_moment / (jnp.sqrt(second_moment) + 1e-08)
    here, params_here = update.shape
    features_total = col_seeds.shape[0]
    owners, cycle = lax.axis_size("param"), lax.axis_size("ex")
    pairs = cycle // 2
    width = features_total // (2 * owners)
    f32 = lambda *shape: jax.ShapeDtypeStruct(shape, jnp.float32)

    other = swap(update, "ex", 1)
    both = pl.pallas_call(
        gather_kernel, out_shape=jax.ShapeDtypeStruct((2 * here, params_here), jnp.bfloat16), name="gather"
    )(update, other)
    rows = jnp.broadcast_to(row_seeds[:, None], (params_here, 128))
    cols = col_seeds.reshape(2 * owners, width)

    inner = owners // 8
    spare = owners.bit_length() - 4

    def blocks(bits):
        order = []
        for index in range(inner):
            high = 0
            for level in range(spare):
                high |= (index >> (spare - 1 - level) & 1) << level
            order.append(bits | high << 3)
        return pl.pallas_call(
            functools.partial(project_kernel, order=tuple(order), depth=min(1024, params_here)),
            out_shape=f32(inner, 2 * here, width),
            name=f"project{bits}",
        )(both, rows, cols)

    sent_x = {bits: swap(blocks(1 | bits), "param", 1) for bits in (6, 4, 2, 0)}
    near = {bits: swap(blocks(2 | bits) + sent_x[2 | bits], "param", 2) for bits in (4, 0)}
    far = swap(blocks(4) + sent_x[4] + near[4], "param", 4)
    pieces = [blocks(0), sent_x[0], near[0], far]
    for level in range(spare):
        half = pieces[0].shape[0] // 2
        total = pieces[0] + pieces[1] + pieces[2] + pieces[3]
        zero = jnp.zeros_like(total[:half])
        pieces = [total[:half], swap(total[half:], "param", 8 << level), zero, zero]

    projected, squares = pl.pallas_call(
        square_kernel, out_shape=(f32(2 * here, width), f32(8, 2 * here)), name="square"
    )(*pieces)
    others = []
    for shift in range(1, pairs):
        perm = [(i, (i - 2 * shift) % cycle) for i in range(cycle)]
        others.append(lax.ppermute(projected, "ex", perm))
    everywhere = jnp.broadcast_to(squares[None], (owners * cycle,) + squares.shape)
    squares_all = lax.all_to_all(everywhere, ("param", "ex"), split_axis=0, concat_axis=0, tiled=True)
    own_features, send_features, own_scores, send_scores = pl.pallas_call(
        functools.partial(score_kernel, features_total=features_total),
        out_shape=(f32(here, width), f32(here, width), f32(here // 2, 2 * LANES), f32(here // 2, 2 * LANES)),
        scratch_shapes=[pltpu.VMEM((8 * pairs, 2 * here), jnp.float32)],
        name="score",
    )(squares_all, group_of.reshape(pairs, 2 * here), projected, *others)
    partial = own_scores + swap(send_scores, "ex", 1)
    partial = jnp.broadcast_to(partial[None], (owners,) + partial.shape)
    partial = lax.all_to_all(partial, "param", split_axis=0, concat_axis=0, tiled=True)
    scores = pl.pallas_call(finish_kernel, out_shape=f32(here, GROUPS), name="finish")(partial)
    received = swap(send_features, "ex", 1)
    first = lax.axis_index("ex") % 2 == 0
    features = jnp.concatenate(
        [jnp.where(first, own_features, received), jnp.where(first, received, own_features)], axis=1
    )
    return (features, scores)


def solution(mesh):
    in_specs = (P("ex", "param"), P("param"), P("param"), P("param"), P(), P())
    out_specs = (P("ex", "param"), P("ex", None))
    return jax.shard_map(shards, mesh=mesh, in_specs=in_specs, out_specs=out_specs, check_vma=False)
```

```python
import functools
import jax
import jax.numpy as jnp
from jax import lax
from jax.experimental import pallas as pl
from jax.experimental.pallas import tpu as pltpu
from jax.sharding import PartitionSpec as P

GROUPS = 57
LANES = 64
SMALL = pltpu.CompilerParams(vmem_limit_bytes=16 << 20)
HIGHEST = lax.Precision.HIGHEST


def swap(value, axis, bits):
    return lax.ppermute(value, axis, [(i, i ^ bits) for i in range(lax.axis_size(axis))])


def wrapped(value):
    value &= 0xFFFFFFFF
    return jnp.int32(value - (1 << 32) if value >> 31 else value)


def negative(row_part, col_part):
    hashed = row_part * col_part
    hashed = hashed ^ hashed >> 15
    hashed = hashed * wrapped(739982445 << 7)
    hashed = hashed ^ hashed << 13
    return (hashed < 0).astype(jnp.bfloat16)


def gather_kernel(own_ref, other_ref, both_ref, sums_ref):
    here = own_ref.shape[0]
    side = lax.axis_index("ex") % 2
    for source, position in ((own_ref, side), (other_ref, 1 - side)):
        value = source[...]
        at = pl.ds(pl.multiple_of(position * here, here), here)
        both_ref[at, :] = value
        sums = jnp.sum(value.astype(jnp.float32), axis=1, keepdims=True)
        sums_ref[at, :] = jnp.broadcast_to(sums, (here, 128))


def columns(cols_ref, at, left, strip, width):
    if width % 128:
        return cols_ref[pl.ds(at, 1), left : left + strip]
    first = at * (width // 128) + left // 128
    return jnp.concatenate([cols_ref[pl.ds(first + i, 1), :] for i in range(strip // 128)], axis=1)


def project_kernel(update_ref, sums_ref, rows_ref, cols_ref, *out_refs, order, depth):
    own = lax.axis_index("param")
    side = lax.axis_index("ex") % 2
    width = out_refs[0].shape[2]
    strip = min(width, 256)
    for slot, relative in enumerate(order):
        at = (own ^ relative) * 2 + side
        for left in range(0, width, strip):
            cols = columns(cols_ref, at, left, strip, width)
            total = None
            for begin in range(0, update_ref.shape[1], depth):
                seeds = rows_ref[begin : begin + depth, :]
                seeds = jnp.tile(seeds, (1, strip // 128)) if strip > 128 else seeds[:, :strip]
                part = jnp.dot(
                    update_ref[:, begin : begin + depth],
                    negative(seeds, cols),
                    preferred_element_type=jnp.float32,
                )
                total = part if total is None else total + part
            total = sums_ref[:, :1] - 2.0 * total
            top = 0
            for out_ref in out_refs:
                bottom = top + out_ref.shape[1]
                out_ref[slot, :, left : left + strip] = total[top:bottom]
                top = bottom


def square_kernel(a_ref, b_ref, c_ref, *refs):
    *last_refs, projected_ref, squares_ref = refs
    last = jnp.concatenate([last_ref[0] for last_ref in last_refs], axis=0)
    projected = a_ref[0] + b_ref[0] + c_ref[0] + last
    projected_ref[...] = projected
    ones = jnp.ones((8, projected.shape[1]), jnp.float32)
    squares = lax.dot_general(
        ones, projected * projected, (((1,), (1,)), ((), ())), precision=HIGHEST
    )
    squares_ref[...] = jnp.broadcast_to(squares[None], squares_ref.shape)


def gram_kernel(*refs):
    *half_refs, out_ref = refs
    here = half_refs[0].shape[0] // 2
    side = lax.axis_index("ex") % 2
    at = pl.ds(pl.multiple_of(side * here, here), here)
    own = [ref[at, :] for ref in half_refs[:2]]
    for index in range(len(half_refs) // 2):
        products = [
            lax.dot_general(mine, ref[...], (((1,), (1,)), ((), ())), precision=HIGHEST)
            for mine, ref in zip(own, half_refs[2 * index : 2 * index + 2])
        ]
        out_ref[index] = products[0] + products[1]


def score_kernel(squares_ref, groups_ref, near_ref, far_ref, gram_ref, feat_ref, score_ref, roots, *, features_total):
    rows, width = near_ref.shape
    here = rows // 2
    pairs = gram_ref.shape[0]
    me = lax.axis_index("ex")
    pair, side = me // 2, me % 2
    for y in range(pairs):
        total = jnp.zeros((8, rows), jnp.float32)
        for slot in range(squares_ref.shape[0]):
            if slot % (2 * pairs) // 2 == y:
                total = total + squares_ref[slot]
        roots[y * 8 : y * 8 + 8, :] = jnp.sqrt(total * (1.0 / features_total) + 1e-06)
    row = roots[pl.ds(pl.multiple_of(pair * 8, 8), 1), :]
    both = jnp.transpose(jnp.broadcast_to(row, (rows, rows)))
    column = jnp.where(side == 0, both[:here, :1], both[here:, :1])
    summed = jnp.zeros((here, LANES), jnp.float32)
    counts = jnp.zeros((8, LANES), jnp.float32)
    for shift in range(pairs):
        there = (pair + shift) % pairs
        products = gram_ref[shift] / roots[pl.ds(pl.multiple_of(there * 8, 8), 1), :]
        groups = groups_ref[pl.ds(there, 1), :]
        onehot = (lax.broadcasted_iota(jnp.int32, (LANES, rows), 0) == groups).astype(jnp.float32)
        summed = summed + lax.dot_general(products, onehot, (((1,), (1,)), ((), ())), precision=HIGHEST)
        counts = counts + lax.dot_general(
            jnp.ones((8, rows), jnp.float32), onehot, (((1,), (1,)), ((), ())), precision=HIGHEST
        )
    scores = summed / column / (jnp.maximum(counts[:1], 1.0) * features_total)
    packed = jnp.concatenate([scores[: here // 2], scores[here // 2 :]], axis=1)
    score_ref[...] = jnp.broadcast_to(packed[None], score_ref.shape)
    at = pl.ds(pl.multiple_of(side * here, here), here)
    near, far = near_ref[at, :] / column, far_ref[at, :] / column
    feat_ref[:, :width] = jnp.where(side == 0, near, far)
    feat_ref[:, width:] = jnp.where(side == 0, far, near)


def finish_kernel(score_ref, out_ref):
    half = score_ref.shape[1]
    total = score_ref[0]
    for slot in range(1, score_ref.shape[0]):
        total = total + score_ref[slot]
    out_ref[:half, :] = total[:, :GROUPS]
    out_ref[half:, :] = total[:, LANES : LANES + GROUPS]


def shards(gradients, m_state, v_state, row_seeds, col_seeds, group_of):
    def updated(first, second, values):
        first_moment = first[None, :] + 0.1 * values
        second_moment = second[None, :] + 0.001 * values * values
        return (first_moment / (jnp.sqrt(second_moment) + 1e-08)).astype(jnp.bfloat16)

    here, params_here = gradients.shape
    features_total = col_seeds.shape[0]
    owners, cycle = lax.axis_size("param"), lax.axis_size("ex")
    pairs = cycle // 2
    width = features_total // (2 * owners)
    f32 = lambda *shape: jax.ShapeDtypeStruct(shape, jnp.float32)

    other = swap(gradients, "ex", 1)
    first, second = 0.9 * m_state, 0.999 * v_state
    own_update = updated(first, second, gradients)
    other_update = updated(*lax.optimization_barrier((first, second, other)))
    both, sums = pl.pallas_call(
        gather_kernel,
        out_shape=(jax.ShapeDtypeStruct((2 * here, params_here), jnp.bfloat16), f32(2 * here, 128)),
        name="gather",
        compiler_params=SMALL,
    )(own_update, other_update)
    rows = jnp.broadcast_to(row_seeds[:, None], (params_here, 128))
    cols = col_seeds.reshape(-1, width if width % 128 else 128)

    inner = owners // 8
    spare = owners.bit_length() - 4

    def blocks(bits, parts):
        order = []
        for index in range(inner):
            high = 0
            for level in range(spare):
                high |= (index >> (spare - 1 - level) & 1) << level
            order.append(bits | high << 3)
        return pl.pallas_call(
            functools.partial(project_kernel, order=tuple(order), depth=min(1024, params_here)),
            out_shape=[f32(inner, 2 * here // parts, width)] * parts,
            compiler_params=SMALL,
        )(both, sums, rows, cols)

    def moved(values, bits):
        out = []
        for value in values:
            out.append(swap(value, "param", bits))
        return out

    def plus(*lists):
        return [functools.reduce(jnp.add, terms) for terms in zip(*lists)]

    x6 = moved(blocks(7, 2), 1)
    x4 = moved(blocks(5, 2), 1)
    x2 = moved(blocks(3, 1), 1)
    x0 = moved(blocks(1, 1), 1)
    n4 = moved(plus(blocks(6, 2), x6), 2)
    n0 = moved(plus(blocks(2, 1), x2), 2)
    far = moved(plus(blocks(4, 2), x4, n4), 4)
    pieces = [*blocks(0, 1), *x0, *n0, *far]
    for level in range(spare):
        half = pieces[0].shape[0] // 2
        last = jnp.concatenate(pieces[3:], axis=1)
        total = pieces[0] + pieces[1] + pieces[2] + last
        zero = jnp.zeros_like(total[:half])
        pieces = [total[:half], swap(total[half:], "param", 8 << level), zero, zero]

    projected, everywhere = pl.pallas_call(
        square_kernel,
        out_shape=(f32(2 * here, width), f32(owners * cycle, 8, 2 * here)),
        name="square",
        compiler_params=SMALL,
    )(*pieces)
    squares = lax.all_to_all(everywhere, ("param", "ex"), split_axis=0, concat_axis=0, tiled=True)
    halves = [projected, swap(projected, "ex", 1)]
    for shift in range(1, pairs):
        there = lax.ppermute(projected, "ex", [(i, (i - 2 * shift) % cycle) for i in range(cycle)])
        halves += [there, swap(there, "ex", 1)]
    gram = pl.pallas_call(
        gram_kernel, out_shape=f32(pairs, here, 2 * here), name="gram", compiler_params=SMALL
    )(*halves)
    features, partial = pl.pallas_call(
        functools.partial(score_kernel, features_total=features_total),
        out_shape=(f32(here, 2 * width), f32(owners, here // 2, 2 * LANES)),
        scratch_shapes=[pltpu.VMEM((8 * pairs, 2 * here), jnp.float32)],
        name="score",
        compiler_params=SMALL,
    )(squares, group_of.reshape(pairs, 2 * here), halves[0], halves[1], gram)
    partial = lax.all_to_all(partial, "param", split_axis=0, concat_axis=0, tiled=True)
    scores = pl.pallas_call(
        finish_kernel, out_shape=f32(here, GROUPS), name="finish", compiler_params=SMALL
    )(partial)
    return (features, scores)


def solution(mesh):
    in_specs = (P("ex", "param"), P("param"), P("param"), P("param"), P(), P())
    out_specs = (P("ex", "param"), P("ex", None))
    return jax.shard_map(shards, mesh=mesh, in_specs=in_specs, out_specs=out_specs, check_vma=False)
```

```python
import functools
import jax
import jax.numpy as jnp
from jax import lax
from jax.experimental import pallas as pl
from jax.experimental.pallas import tpu as pltpu
from jax.sharding import PartitionSpec as P

GROUPS = 57
LANES = 64
SMALL = pltpu.CompilerParams(vmem_limit_bytes=16 << 20)
HIGHEST = lax.Precision.HIGHEST


def swap(value, axis, bits):
    return lax.ppermute(value, axis, [(i, i ^ bits) for i in range(lax.axis_size(axis))])


def wrapped(value):
    value &= 0xFFFFFFFF
    return jnp.int32(value - (1 << 32) if value >> 31 else value)


def negative(row_part, col_part):
    hashed = row_part * col_part
    hashed = hashed ^ hashed >> 15
    hashed = hashed * wrapped(739982445 << 7)
    hashed = hashed ^ hashed << 13
    return (hashed < 0).astype(jnp.bfloat16)


def gather_kernel(own_ref, other_ref, both_ref, sums_ref):
    here = own_ref.shape[0]
    side = lax.axis_index("ex") % 2
    for source, position in ((own_ref, side), (other_ref, 1 - side)):
        value = source[...]
        at = pl.ds(pl.multiple_of(position * here, here), here)
        both_ref[at, :] = value
        sums = jnp.sum(value.astype(jnp.float32), axis=1, keepdims=True)
        sums_ref[at, :] = jnp.broadcast_to(sums, (here, 128))


def columns(cols_ref, at, left, strip, width):
    if width % 128:
        return cols_ref[pl.ds(at, 1), left : left + strip]
    first = at * (width // 128) + left // 128
    return jnp.concatenate([cols_ref[pl.ds(first + i, 1), :] for i in range(strip // 128)], axis=1)


def project_kernel(update_ref, sums_ref, rows_ref, cols_ref, *out_refs, order, depth):
    own = lax.axis_index("param")
    side = lax.axis_index("ex") % 2
    width = out_refs[0].shape[2]
    strip = min(width, 256)
    for slot, relative in enumerate(order):
        at = (own ^ relative) * 2 + side
        for left in range(0, width, strip):
            cols = columns(cols_ref, at, left, strip, width)
            total = None
            for begin in range(0, update_ref.shape[1], depth):
                seeds = rows_ref[begin : begin + depth, :]
                seeds = jnp.tile(seeds, (1, strip // 128)) if strip > 128 else seeds[:, :strip]
                part = jnp.dot(
                    update_ref[:, begin : begin + depth],
                    negative(seeds, cols),
                    preferred_element_type=jnp.float32,
                )
                total = part if total is None else total + part
            total = sums_ref[:, :1] - 2.0 * total
            top = 0
            for out_ref in out_refs:
                bottom = top + out_ref.shape[1]
                out_ref[slot, :, left : left + strip] = total[top:bottom]
                top = bottom


def square_kernel(*refs):
    *piece_refs, projected_ref, squares_ref = refs
    rows = projected_ref.shape[0]
    projected, part = None, []
    for ref in piece_refs:
        part.append(ref[0])
        if sum(p.shape[0] for p in part) == rows:
            piece = jnp.concatenate(part, axis=0) if len(part) > 1 else part[0]
            projected, part = piece if projected is None else projected + piece, []
    projected_ref[...] = projected
    ones = jnp.ones((8, projected.shape[1]), jnp.float32)
    squares = lax.dot_general(
        ones, projected * projected, (((1,), (1,)), ((), ())), precision=HIGHEST
    )
    squares_ref[...] = jnp.broadcast_to(squares[None, :1], squares_ref.shape)


def gram_kernel(*refs):
    *half_refs, out_ref = refs
    here = half_refs[0].shape[0] // 2
    side = lax.axis_index("ex") % 2
    at = pl.ds(pl.multiple_of(side * here, here), here)
    own = [ref[at, :] for ref in half_refs[:2]]
    for index in range(len(half_refs) // 2):
        products = [
            lax.dot_general(mine, ref[...], (((1,), (1,)), ((), ())), precision=HIGHEST)
            for mine, ref in zip(own, half_refs[2 * index : 2 * index + 2])
        ]
        out_ref[index] = products[0] + products[1]


def score_kernel(squares_ref, groups_ref, near_ref, far_ref, gram_ref, feat_ref, score_ref, roots, *, features_total):
    rows, width = near_ref.shape
    here = rows // 2
    pairs = gram_ref.shape[0]
    me = lax.axis_index("ex")
    pair, side = me // 2, me % 2
    for y in range(pairs):
        total = jnp.zeros((1, rows), jnp.float32)
        for slot in range(squares_ref.shape[0]):
            if slot % (2 * pairs) // 2 == y:
                total = total + squares_ref[slot]
        roots[y : y + 1, :] = jnp.sqrt(total * (1.0 / features_total) + 1e-06)
    row = roots[pl.ds(pair, 1), :]
    both = jnp.transpose(jnp.broadcast_to(row, (rows, rows)))
    column = jnp.where(side == 0, both[:here, :1], both[here:, :1])
    summed = jnp.zeros((here, LANES), jnp.float32)
    counts = jnp.zeros((8, LANES), jnp.float32)
    for shift in range(pairs):
        there = (pair + shift) % pairs
        products = gram_ref[shift] / roots[pl.ds(there, 1), :]
        groups = groups_ref[pl.ds(there, 1), :]
        onehot = (lax.broadcasted_iota(jnp.int32, (LANES, rows), 0) == groups).astype(jnp.float32)
        summed = summed + lax.dot_general(products, onehot, (((1,), (1,)), ((), ())), precision=HIGHEST)
        counts = counts + lax.dot_general(
            jnp.ones((8, rows), jnp.float32), onehot, (((1,), (1,)), ((), ())), precision=HIGHEST
        )
    scores = summed / column / (jnp.maximum(counts[:1], 1.0) * features_total)
    packed = jnp.concatenate([scores[: here // 2], scores[here // 2 :]], axis=1)
    score_ref[...] = jnp.broadcast_to(packed[None], score_ref.shape)
    at = pl.ds(pl.multiple_of(side * here, here), here)
    near, far = near_ref[at, :] / column, far_ref[at, :] / column
    feat_ref[:, :width] = jnp.where(side == 0, near, far)
    feat_ref[:, width:] = jnp.where(side == 0, far, near)


def finish_kernel(score_ref, out_ref):
    half = score_ref.shape[1]
    total = score_ref[0]
    for slot in range(1, score_ref.shape[0]):
        total = total + score_ref[slot]
    out_ref[:half, :] = total[:, :GROUPS]
    out_ref[half:, :] = total[:, LANES : LANES + GROUPS]


def shards(gradients, m_state, v_state, row_seeds, col_seeds, group_of):
    def updated(first, second, values):
        first_moment = first[None, :] + 0.1 * values
        second_moment = second[None, :] + 0.001 * values * values
        return (first_moment / (jnp.sqrt(second_moment) + 1e-08)).astype(jnp.bfloat16)

    here, params_here = gradients.shape
    features_total = col_seeds.shape[0]
    owners, cycle = lax.axis_size("param"), lax.axis_size("ex")
    pairs = cycle // 2
    width = features_total // (2 * owners)
    f32 = lambda *shape: jax.ShapeDtypeStruct(shape, jnp.float32)

    other = swap(gradients, "ex", 1)
    first, second = 0.9 * m_state, 0.999 * v_state
    own_update = updated(first, second, gradients)
    other_update = updated(*lax.optimization_barrier((first, second, other)))
    both, sums = pl.pallas_call(
        gather_kernel,
        out_shape=(jax.ShapeDtypeStruct((2 * here, params_here), jnp.bfloat16), f32(2 * here, 128)),
        name="gather",
        compiler_params=SMALL,
    )(own_update, other_update)
    rows = jnp.broadcast_to(row_seeds[:, None], (params_here, 128))
    cols = col_seeds.reshape(-1, width if width % 128 else 128)

    inner = owners // 8
    spare = owners.bit_length() - 4

    def blocks(bits, parts):
        order = []
        for index in range(inner):
            high = 0
            for level in range(spare):
                high |= (index >> (spare - 1 - level) & 1) << level
            order.append(bits | high << 3)
        return pl.pallas_call(
            functools.partial(project_kernel, order=tuple(order), depth=min(1024, params_here)),
            out_shape=[f32(inner, 2 * here // parts, width)] * parts,
            compiler_params=SMALL,
        )(both, sums, rows, cols)

    def moved(values, bits):
        out = []
        for value in values:
            out.append(swap(value, "param", bits))
        return out

    def cut(values, parts):
        if len(values) == parts:
            return values
        if len(values) > parts:
            return [jnp.concatenate(values, axis=1)]
        size = 2 * here // parts
        return [values[0][:, i * size : (i + 1) * size] for i in range(parts)]

    def plus(parts, *lists):
        return [functools.reduce(jnp.add, terms) for terms in zip(*(cut(values, parts) for values in lists))]

    n7 = moved(blocks(7, 1), 2)
    x3 = moved(blocks(3, 1), 1)
    n6 = moved(blocks(6, 1), 2)
    x5 = moved(plus(2, blocks(5, 2), n7), 1)
    n2 = moved(plus(1, blocks(2, 1), x3), 2)
    x1 = moved(blocks(1, 1), 1)
    far = moved(plus(2, blocks(4, 2), n6, x5), 4)
    pieces = [blocks(0, 1), x1, n2, far]
    for level in range(spare):
        (total,) = plus(1, *pieces)
        half = total.shape[0] // 2
        pieces = [[total[:half]], [swap(total[half:], "param", 8 << level)]]

    projected, everywhere = pl.pallas_call(
        square_kernel,
        out_shape=(f32(2 * here, width), f32(owners * cycle, 1, 2 * here)),
        name="square",
        compiler_params=SMALL,
    )(*(value for piece in pieces for value in piece))
    squares = lax.all_to_all(everywhere, ("param", "ex"), split_axis=0, concat_axis=0, tiled=True)
    halves = [projected, swap(projected, "ex", 1)]
    for shift in range(1, pairs):
        there = lax.ppermute(projected, "ex", [(i, (i - 2 * shift) % cycle) for i in range(cycle)])
        halves += [there, swap(there, "ex", 1)]
    gram = pl.pallas_call(
        gram_kernel, out_shape=f32(pairs, here, 2 * here), name="gram", compiler_params=SMALL
    )(*halves)
    features, partial = pl.pallas_call(
        functools.partial(score_kernel, features_total=features_total),
        out_shape=(f32(here, 2 * width), f32(owners, here // 2, 2 * LANES)),
        scratch_shapes=[pltpu.VMEM((pairs, 2 * here), jnp.float32)],
        name="score",
        compiler_params=SMALL,
    )(squares, group_of.reshape(pairs, 2 * here), halves[0], halves[1], gram)
    partial = lax.all_to_all(partial, "param", split_axis=0, concat_axis=0, tiled=True)
    scores = pl.pallas_call(
        finish_kernel, out_shape=f32(here, GROUPS), name="finish", compiler_params=SMALL
    )(partial)
    return (features, scores)


def solution(mesh):
    in_specs = (P("ex", "param"), P("param"), P("param"), P("param"), P(), P())
    out_specs = (P("ex", "param"), P("ex", None))
    return jax.shard_map(shards, mesh=mesh, in_specs=in_specs, out_specs=out_specs, check_vma=False)
```

```python
import functools
import jax
import jax.numpy as jnp
from jax import lax
from jax.experimental import pallas as pl
from jax.experimental.pallas import tpu as pltpu
from jax.sharding import PartitionSpec as P

GROUPS = 57
LANES = 64
SMALL = pltpu.CompilerParams(vmem_limit_bytes=16 << 20)
HIGHEST = lax.Precision.HIGHEST


def swap(value, axis, bits):
    return lax.ppermute(value, axis, [(i, i ^ bits) for i in range(lax.axis_size(axis))])


def wrapped(value):
    value &= 0xFFFFFFFF
    return jnp.int32(value - (1 << 32) if value >> 31 else value)


def negative(row_part, col_part):
    hashed = row_part * col_part
    hashed = hashed ^ hashed >> 15
    hashed = hashed * wrapped(739982445 << 7)
    hashed = hashed ^ hashed << 13
    return (hashed < 0).astype(jnp.bfloat16)


def gather_kernel(own_ref, other_ref, both_ref, sums_ref):
    here = own_ref.shape[0]
    side = lax.axis_index("ex") % 2
    for source, position in ((own_ref, side), (other_ref, 1 - side)):
        value = source[...]
        at = pl.ds(pl.multiple_of(position * here, here), here)
        both_ref[at, :] = value
        sums = jnp.sum(value.astype(jnp.float32), axis=1, keepdims=True)
        sums_ref[at, :] = jnp.broadcast_to(sums, (here, 128))


def columns(cols_ref, at, left, strip, width):
    if width % 128:
        return cols_ref[pl.ds(at, 1), left : left + strip]
    first = at * (width // 128) + left // 128
    return jnp.concatenate([cols_ref[pl.ds(first + i, 1), :] for i in range(strip // 128)], axis=1)


def project_kernel(update_ref, sums_ref, rows_ref, cols_ref, *out_refs, order, depth):
    own = lax.axis_index("param")
    side = lax.axis_index("ex") % 2
    width = out_refs[0].shape[2]
    strip = min(width, 256)
    for slot, relative in enumerate(order):
        at = (own ^ relative) * 2 + side
        for left in range(0, width, strip):
            cols = columns(cols_ref, at, left, strip, width)
            total = None
            for begin in range(0, update_ref.shape[1], depth):
                seeds = rows_ref[begin : begin + depth, :]
                seeds = jnp.tile(seeds, (1, strip // 128)) if strip > 128 else seeds[:, :strip]
                part = jnp.dot(
                    update_ref[:, begin : begin + depth],
                    negative(seeds, cols),
                    preferred_element_type=jnp.float32,
                )
                total = part if total is None else total + part
            total = sums_ref[:, :1] - 2.0 * total
            top = 0
            for out_ref in out_refs:
                bottom = top + out_ref.shape[1]
                out_ref[slot, :, left : left + strip] = total[top:bottom]
                top = bottom


def square_kernel(*refs):
    *piece_refs, projected_ref, squares_ref = refs
    rows = projected_ref.shape[0]
    projected, part = None, []
    for ref in piece_refs:
        part.append(ref[0])
        if sum(p.shape[0] for p in part) == rows:
            piece = jnp.concatenate(part, axis=0) if len(part) > 1 else part[0]
            projected, part = piece if projected is None else projected + piece, []
    projected_ref[...] = projected
    squares = jnp.sum(projected * projected, axis=1, keepdims=True)
    squares = jnp.transpose(jnp.broadcast_to(squares, (rows, rows)))[:1]
    squares_ref[...] = jnp.broadcast_to(squares[None], squares_ref.shape)


def gram_kernel(groups_ref, *refs, features_total):
    *half_refs, out_ref, onehot_ref, scale_ref = refs
    here = half_refs[0].shape[0] // 2
    side = lax.axis_index("ex") % 2
    at = pl.ds(pl.multiple_of(side * here, here), here)
    own = [ref[at, :] for ref in half_refs[:2]]
    for index in range(len(half_refs) // 2):
        products = [
            lax.dot_general(mine, ref[...], (((1,), (1,)), ((), ())), precision=HIGHEST)
            for mine, ref in zip(own, half_refs[2 * index : 2 * index + 2])
        ]
        out_ref[index] = products[0] + products[1]
    pairs, rows = groups_ref.shape
    pair = lax.axis_index("ex") // 2
    counts = jnp.zeros((8, LANES), jnp.float32)
    for shift in range(pairs):
        groups = groups_ref[pl.ds((pair + shift) % pairs, 1), :]
        onehot = (lax.broadcasted_iota(jnp.int32, (LANES, rows), 0) == groups).astype(jnp.float32)
        onehot_ref[shift] = onehot
        counts = counts + lax.dot_general(
            jnp.ones((8, rows), jnp.float32), onehot, (((1,), (1,)), ((), ())), precision=HIGHEST
        )
    scale_ref[...] = jnp.maximum(counts, 1.0) * features_total


def score_kernel(squares_ref, onehot_ref, scale_ref, near_ref, far_ref, gram_ref, feat_ref, score_ref, roots, *, features_total):
    rows, width = near_ref.shape
    here = rows // 2
    pairs = gram_ref.shape[0]
    me = lax.axis_index("ex")
    pair, side = me // 2, me % 2
    for y in range(pairs):
        total = jnp.zeros((1, rows), jnp.float32)
        for slot in range(squares_ref.shape[0]):
            if slot % (2 * pairs) // 2 == y:
                total = total + squares_ref[slot]
        roots[y : y + 1, :] = jnp.sqrt(total * (1.0 / features_total) + 1e-06)
    row = roots[pl.ds(pair, 1), :]
    both = jnp.transpose(jnp.broadcast_to(row, (rows, rows)))
    column = jnp.where(side == 0, both[:here, :1], both[here:, :1])
    summed = jnp.zeros((here, LANES), jnp.float32)
    for shift in range(pairs):
        there = (pair + shift) % pairs
        products = gram_ref[shift] / roots[pl.ds(there, 1), :]
        summed = summed + lax.dot_general(
            products, onehot_ref[shift], (((1,), (1,)), ((), ())), precision=HIGHEST
        )
    scores = summed / column / scale_ref[:1]
    packed = jnp.concatenate([scores[: here // 2], scores[here // 2 :]], axis=1)
    score_ref[...] = jnp.broadcast_to(packed[None], score_ref.shape)
    at = pl.ds(pl.multiple_of(side * here, here), here)
    near, far = near_ref[at, :] / column, far_ref[at, :] / column
    feat_ref[:, :width] = jnp.where(side == 0, near, far)
    feat_ref[:, width:] = jnp.where(side == 0, far, near)


def finish_kernel(score_ref, out_ref):
    half = score_ref.shape[1]
    total = score_ref[0]
    for slot in range(1, score_ref.shape[0]):
        total = total + score_ref[slot]
    out_ref[:half, :] = total[:, :GROUPS]
    out_ref[half:, :] = total[:, LANES : LANES + GROUPS]


def shards(gradients, m_state, v_state, row_seeds, col_seeds, group_of):
    def updated(first, second, values):
        first_moment = first[None, :] + 0.1 * values
        second_moment = second[None, :] + 0.001 * values * values
        return (first_moment / (jnp.sqrt(second_moment) + 1e-08)).astype(jnp.bfloat16)

    here, params_here = gradients.shape
    features_total = col_seeds.shape[0]
    owners, cycle = lax.axis_size("param"), lax.axis_size("ex")
    pairs = cycle // 2
    width = features_total // (2 * owners)
    f32 = lambda *shape: jax.ShapeDtypeStruct(shape, jnp.float32)

    other = swap(gradients, "ex", 1)
    first, second = 0.9 * m_state, 0.999 * v_state
    own_update = updated(first, second, gradients)
    other_update = updated(*lax.optimization_barrier((first, second, other)))
    both, sums = pl.pallas_call(
        gather_kernel,
        out_shape=(jax.ShapeDtypeStruct((2 * here, params_here), jnp.bfloat16), f32(2 * here, 128)),
        name="gather",
        compiler_params=SMALL,
    )(own_update, other_update)
    rows = jnp.broadcast_to(row_seeds[:, None], (params_here, 128))
    cols = col_seeds.reshape(-1, width if width % 128 else 128)

    inner = owners // 8
    spare = owners.bit_length() - 4

    def blocks(bits, parts):
        order = []
        for index in range(inner):
            high = 0
            for level in range(spare):
                high |= (index >> (spare - 1 - level) & 1) << level
            order.append(bits | high << 3)
        return pl.pallas_call(
            functools.partial(project_kernel, order=tuple(order), depth=min(1024, params_here)),
            out_shape=[f32(inner, 2 * here // parts, width)] * parts,
            compiler_params=SMALL,
        )(both, sums, rows, cols)

    def moved(values, bits):
        out = []
        for value in values:
            out.append(swap(value, "param", bits))
        return out

    def cut(values, parts):
        if len(values) == parts:
            return values
        if len(values) > parts:
            return [jnp.concatenate(values, axis=1)]
        size = 2 * here // parts
        return [values[0][:, i * size : (i + 1) * size] for i in range(parts)]

    def plus(parts, *lists):
        return [functools.reduce(jnp.add, terms) for terms in zip(*(cut(values, parts) for values in lists))]

    n7 = moved(blocks(7, 1), 2)
    x3 = moved(blocks(3, 1), 1)
    n6 = moved(blocks(6, 1), 2)
    x5 = moved(plus(2, blocks(5, 2), n7), 1)
    n2 = moved(plus(1, blocks(2, 1), x3), 2)
    x1 = moved(blocks(1, 1), 1)
    far = moved(plus(2, blocks(4, 2), n6, x5), 4)
    pieces = [blocks(0, 1), x1, n2, far]
    for level in range(spare):
        (total,) = plus(1, *pieces)
        half = total.shape[0] // 2
        pieces = [[total[:half]], [swap(total[half:], "param", 8 << level)]]

    projected, everywhere = pl.pallas_call(
        square_kernel,
        out_shape=(f32(2 * here, width), f32(owners * cycle, 1, 2 * here)),
        name="square",
        compiler_params=SMALL,
    )(*(value for piece in pieces for value in piece))
    squares = lax.all_to_all(everywhere, ("param", "ex"), split_axis=0, concat_axis=0, tiled=True)
    halves = [projected, swap(projected, "ex", 1)]
    for shift in range(1, pairs):
        there = lax.ppermute(projected, "ex", [(i, (i - 2 * shift) % cycle) for i in range(cycle)])
        halves += [there, swap(there, "ex", 1)]
    gram, onehot, scale = pl.pallas_call(
        functools.partial(gram_kernel, features_total=features_total),
        out_shape=(f32(pairs, here, 2 * here), f32(pairs, LANES, 2 * here), f32(8, LANES)),
        name="gram",
        compiler_params=SMALL,
    )(group_of.reshape(pairs, 2 * here), *halves)
    features, partial = pl.pallas_call(
        functools.partial(score_kernel, features_total=features_total),
        out_shape=(f32(here, 2 * width), f32(owners, here // 2, 2 * LANES)),
        scratch_shapes=[pltpu.VMEM((pairs, 2 * here), jnp.float32)],
        name="score",
        compiler_params=SMALL,
    )(squares, onehot, scale, halves[0], halves[1], gram)
    partial = lax.all_to_all(partial, "param", split_axis=0, concat_axis=0, tiled=True)
    scores = pl.pallas_call(
        finish_kernel, out_shape=f32(here, GROUPS), name="finish", compiler_params=SMALL
    )(partial)
    return (features, scores)


def solution(mesh):
    in_specs = (P("ex", "param"), P("param"), P("param"), P("param"), P(), P())
    out_specs = (P("ex", "param"), P("ex", None))
    return jax.shard_map(shards, mesh=mesh, in_specs=in_specs, out_specs=out_specs, check_vma=False)
```

```python
import functools
import jax
import jax.numpy as jnp
from jax import lax
from jax.experimental import pallas as pl
from jax.experimental.pallas import tpu as pltpu
from jax.sharding import PartitionSpec as P

GROUPS = 57
LANES = 64
SMALL = pltpu.CompilerParams(vmem_limit_bytes=16 << 20)
DENSE = pltpu.CompilerParams(vmem_limit_bytes=16 << 20)
HIGHEST = lax.Precision.HIGHEST


def swap(value, axis, bits):
    return lax.ppermute(value, axis, [(i, i ^ bits) for i in range(lax.axis_size(axis))])


def wrapped(value):
    value &= 0xFFFFFFFF
    return jnp.int32(value - (1 << 32) if value >> 31 else value)


def negative(row_part, col_part):
    hashed = row_part * col_part
    hashed = hashed ^ hashed >> 15
    hashed = hashed * wrapped(739982445 << 7)
    hashed = hashed ^ hashed << 13
    return (hashed < 0).astype(jnp.bfloat16)


def gather_kernel(own_ref, other_ref, both_ref, sums_ref):
    here = own_ref.shape[0]
    side = lax.axis_index("ex") % 2
    for source, position in ((own_ref, side), (other_ref, 1 - side)):
        value = source[...]
        at = pl.ds(pl.multiple_of(position * here, here), here)
        both_ref[at, :] = value
        sums = jnp.sum(value.astype(jnp.float32), axis=1, keepdims=True)
        sums_ref[at, :] = jnp.broadcast_to(sums, (here, 128))


def columns(cols_ref, at, left, strip, width):
    if width % 128:
        return cols_ref[pl.ds(at, 1), left : left + strip]
    first = at * (width // 128) + left // 128
    return jnp.concatenate([cols_ref[pl.ds(first + i, 1), :] for i in range(strip // 128)], axis=1)


def project_kernel(update_ref, sums_ref, rows_ref, cols_ref, *out_refs, order, depth):
    own = lax.axis_index("param")
    side = lax.axis_index("ex") % 2
    width = out_refs[0].shape[2]
    strip = min(width, 256)
    for slot, relative in enumerate(order):
        at = (own ^ relative) * 2 + side
        for left in range(0, width, strip):
            cols = columns(cols_ref, at, left, strip, width)
            total = None
            for begin in range(0, update_ref.shape[1], depth):
                seeds = rows_ref[begin : begin + depth, :]
                seeds = jnp.tile(seeds, (1, strip // 128)) if strip > 128 else seeds[:, :strip]
                part = jnp.dot(
                    update_ref[:, begin : begin + depth],
                    negative(seeds, cols),
                    preferred_element_type=jnp.float32,
                )
                total = part if total is None else total + part
            total = sums_ref[:, :1] - 2.0 * total
            top = 0
            for out_ref in out_refs:
                bottom = top + out_ref.shape[1]
                out_ref[slot, :, left : left + strip] = total[top:bottom]
                top = bottom


def square_kernel(*refs):
    *piece_refs, projected_ref, squares_ref = refs
    rows = projected_ref.shape[0]
    projected, part = None, []
    for ref in piece_refs:
        part.append(ref[0])
        if sum(p.shape[0] for p in part) == rows:
            piece = jnp.concatenate(part, axis=0) if len(part) > 1 else part[0]
            projected, part = piece if projected is None else projected + piece, []
    projected_ref[...] = projected
    squares = jnp.sum(projected * projected, axis=1, keepdims=True)
    squares = jnp.transpose(jnp.broadcast_to(squares, (rows, rows)))[:1]
    squares_ref[...] = jnp.broadcast_to(squares[None], squares_ref.shape)


def gram_kernel(groups_ref, *refs, features_total):
    *half_refs, out_ref, onehot_ref, scale_ref = refs
    here = half_refs[0].shape[0] // 2
    side = lax.axis_index("ex") % 2
    at = pl.ds(pl.multiple_of(side * here, here), here)
    own = [ref[at, :] for ref in half_refs[:2]]
    for index in range(len(half_refs) // 2):
        products = [
            lax.dot_general(mine, ref[...], (((1,), (1,)), ((), ())), precision=lax.Precision.HIGH)
            for mine, ref in zip(own, half_refs[2 * index : 2 * index + 2])
        ]
        out_ref[index] = products[0] + products[1]
    pairs, rows = groups_ref.shape
    pair = lax.axis_index("ex") // 2
    counts = jnp.zeros((8, LANES), jnp.float32)
    for shift in range(pairs):
        groups = groups_ref[pl.ds((pair + shift) % pairs, 1), :]
        onehot = (lax.broadcasted_iota(jnp.int32, (LANES, rows), 0) == groups).astype(jnp.float32)
        onehot_ref[shift] = onehot
        counts = counts + lax.dot_general(
            jnp.ones((8, rows), jnp.float32), onehot, (((1,), (1,)), ((), ())), precision=HIGHEST
        )
    scale_ref[...] = jnp.maximum(counts, 1.0) * features_total


def score_kernel(squares_ref, onehot_ref, scale_ref, near_ref, far_ref, gram_ref, feat_ref, score_ref, roots, *, features_total):
    rows, width = near_ref.shape
    here = rows // 2
    pairs = gram_ref.shape[0]
    me = lax.axis_index("ex")
    pair, side = me // 2, me % 2
    for y in range(pairs):
        total = jnp.zeros((1, rows), jnp.float32)
        for slot in range(squares_ref.shape[0]):
            if slot % (2 * pairs) // 2 == y:
                total = total + squares_ref[slot]
        roots[y : y + 1, :] = jnp.sqrt(total * (1.0 / features_total) + 1e-06)
    row = roots[pl.ds(pair, 1), :]
    both = jnp.transpose(jnp.broadcast_to(row, (rows, rows)))
    column = jnp.where(side == 0, both[:here, :1], both[here:, :1])
    summed = jnp.zeros((here, LANES), jnp.float32)
    for shift in range(pairs):
        there = (pair + shift) % pairs
        products = gram_ref[shift] / roots[pl.ds(there, 1), :]
        summed = summed + lax.dot_general(
            products, onehot_ref[shift], (((1,), (1,)), ((), ())), precision=HIGHEST
        )
    scores = summed / column / scale_ref[:1]
    packed = jnp.concatenate([scores[: here // 2], scores[here // 2 :]], axis=1)
    score_ref[...] = jnp.broadcast_to(packed[None], score_ref.shape)
    at = pl.ds(pl.multiple_of(side * here, here), here)
    near, far = near_ref[at, :] / column, far_ref[at, :] / column
    feat_ref[:, :width] = jnp.where(side == 0, near, far)
    feat_ref[:, width:] = jnp.where(side == 0, far, near)


def finish_kernel(score_ref, out_ref):
    half = score_ref.shape[1]
    total = score_ref[0]
    for slot in range(1, score_ref.shape[0]):
        total = total + score_ref[slot]
    out_ref[:half, :] = total[:, :GROUPS]
    out_ref[half:, :] = total[:, LANES : LANES + GROUPS]


def shards(gradients, m_state, v_state, row_seeds, col_seeds, group_of):
    def updated(first, second, values):
        first_moment = first[None, :] + 0.1 * values
        second_moment = second[None, :] + 0.001 * values * values
        return (first_moment / (jnp.sqrt(second_moment) + 1e-08)).astype(jnp.bfloat16)

    here, params_here = gradients.shape
    features_total = col_seeds.shape[0]
    owners, cycle = lax.axis_size("param"), lax.axis_size("ex")
    pairs = cycle // 2
    width = features_total // (2 * owners)
    f32 = lambda *shape: jax.ShapeDtypeStruct(shape, jnp.float32)

    other = swap(gradients, "ex", 1)
    first, second = 0.9 * m_state, 0.999 * v_state
    own_update = updated(first, second, gradients)
    other_update = updated(*lax.optimization_barrier((first, second, other)))
    both, sums = pl.pallas_call(
        gather_kernel,
        out_shape=(jax.ShapeDtypeStruct((2 * here, params_here), jnp.bfloat16), f32(2 * here, 128)),
        name="gather",
        compiler_params=SMALL,
    )(own_update, other_update)
    rows = jnp.broadcast_to(row_seeds[:, None], (params_here, 128))
    cols = col_seeds.reshape(-1, width if width % 128 else 128)

    inner = owners // 8
    spare = owners.bit_length() - 4

    def blocks(bits, parts):
        order = []
        for index in range(inner):
            high = 0
            for level in range(spare):
                high |= (index >> (spare - 1 - level) & 1) << level
            order.append(bits | high << 3)
        return pl.pallas_call(
            functools.partial(project_kernel, order=tuple(order), depth=min(1024, params_here)),
            out_shape=[f32(inner, 2 * here // parts, width)] * parts,
            compiler_params=DENSE,
        )(both, sums, rows, cols)

    def moved(values, bits):
        out = []
        for value in values:
            out.append(swap(value, "param", bits))
        return out

    def cut(values, parts):
        if len(values) == parts:
            return values
        if len(values) > parts:
            return [jnp.concatenate(values, axis=1)]
        size = 2 * here // parts
        return [values[0][:, i * size : (i + 1) * size] for i in range(parts)]

    def plus(parts, *lists):
        return [functools.reduce(jnp.add, terms) for terms in zip(*(cut(values, parts) for values in lists))]

    n7 = moved(blocks(7, 1), 2)
    x3 = moved(blocks(3, 1), 1)
    n6 = moved(blocks(6, 1), 2)
    x5 = moved(plus(2, blocks(5, 2), n7), 1)
    n2 = moved(plus(1, blocks(2, 1), x3), 2)
    x1 = moved(blocks(1, 1), 1)
    far = moved(plus(2, blocks(4, 2), n6, x5), 4)
    pieces = [blocks(0, 1), x1, n2, far]
    for level in range(spare):
        (total,) = plus(1, *pieces)
        half = total.shape[0] // 2
        pieces = [[total[:half]], [swap(total[half:], "param", 8 << level)]]

    projected, everywhere = pl.pallas_call(
        square_kernel,
        out_shape=(f32(2 * here, width), f32(owners * cycle, 1, 2 * here)),
        name="square",
        compiler_params=SMALL,
    )(*(value for piece in pieces for value in piece))
    squares = lax.all_to_all(everywhere, ("param", "ex"), split_axis=0, concat_axis=0, tiled=True)
    halves = [projected, swap(projected, "ex", 1)]
    for shift in range(1, pairs):
        there = lax.ppermute(projected, "ex", [(i, (i - 2 * shift) % cycle) for i in range(cycle)])
        halves += [there, swap(there, "ex", 1)]
    gram, onehot, scale = pl.pallas_call(
        functools.partial(gram_kernel, features_total=features_total),
        out_shape=(f32(pairs, here, 2 * here), f32(pairs, LANES, 2 * here), f32(8, LANES)),
        name="gram",
        compiler_params=SMALL,
    )(group_of.reshape(pairs, 2 * here), *halves)
    features, partial = pl.pallas_call(
        functools.partial(score_kernel, features_total=features_total),
        out_shape=(f32(here, 2 * width), f32(owners, here // 2, 2 * LANES)),
        scratch_shapes=[pltpu.VMEM((pairs, 2 * here), jnp.float32)],
        name="score",
        compiler_params=SMALL,
    )(squares, onehot, scale, halves[0], halves[1], gram)
    partial = lax.all_to_all(partial, "param", split_axis=0, concat_axis=0, tiled=True)
    scores = pl.pallas_call(
        finish_kernel, out_shape=f32(here, GROUPS), name="finish", compiler_params=SMALL
    )(partial)
    return (features, scores)


def solution(mesh):
    in_specs = (P("ex", "param"), P("param"), P("param"), P("param"), P(), P())
    out_specs = (P("ex", "param"), P("ex", None))
    return jax.shard_map(shards, mesh=mesh, in_specs=in_specs, out_specs=out_specs, check_vma=False)
```
